1024 devices in a mesh: pipe: 4 (over y), expert: 64 (over z, core), tensor: 4 (over x).
Axes of the slice: x: 4, y: 4, z: 32, core: 2. Of those that a mesh axis runs over, the one named last changes fastest.
Arguments:
- sent_grad: bfloat16 [4, 8192, 3584], P('pipe', 'expert', 'tensor'), may hold values from -4 to 4
- head_grad: bfloat16 [8192, 3584], P('expert', 'tensor'), may hold values from -4 to 4
- probs: bfloat16 [4, 8192, 8], P('pipe', 'expert'), may hold values from 0.049804688 to 1
- expert_ids: int32 [4, 8192, 8], P('pipe', 'expert'), may hold values from 0 to 63, as said below
- hidden_act: bfloat16 [4, 64, 1088, 1024], P('pipe', 'expert', None, 'tensor'), may hold values from -0.1875 to 0.1875
Outputs:
- w_down_grad: bfloat16 [4, 64, 1024, 3584], P('pipe', 'expert', 'tensor')
The draws below stay inside these ranges and needn't reach their ends.
Inputs may be any that keep to these rules, and one draw needn't show every extreme that they name: `expert_ids`: each token names 8 different experts. In each section and each block of 128 tokens one expert is named by exactly 17 pairs, one by 17 - 2 pairs, and every other expert by 17 - 1 pairs.
All inputs are finite; a program needn't handle non-finite values.
Results may differ from the reference program's by a relative error of at most 0.0049.
Values may be sent and summed in bfloat16 or wider, within the bound.
A program may use at most 32 MiB of HBM per device.

```python
import jax
import jax.numpy as jnp
from jax import lax

D = 3584
HID = 1024
EXPERTS = 64
TOPK = 8
TOK = 128
MOST = 17
SLOTS = 1088
TOKENS = 8192
SECTIONS = 4
N_EXPERT = 64


def draw_expert_ids(key, part):
    spread = EXPERTS // TOPK
    blocks = SECTIONS * N_EXPERT
    hot_key, order_key, token_key, choice_key = jax.random.split(key, 4)
    hot = jax.random.randint(hot_key, (SECTIONS,), 0, EXPERTS, dtype=jnp.int32)
    hot_block = jnp.repeat(hot, N_EXPERT)
    order_keys = jax.random.split(order_key, blocks)
    token_keys = jax.random.split(token_key, blocks)
    choice_keys = jax.random.split(choice_key, blocks)

    def one_block(okey, tkey, ckey, hot_one):
        order = jax.random.permutation(okey, EXPERTS).astype(jnp.int32)
        position = jnp.argmax(order == hot_one).astype(jnp.int32)
        token_index = jnp.arange(TOK, dtype=jnp.int32)[:, None]
        column = jnp.arange(TOPK, dtype=jnp.int32)[None, :]
        chosen = order[(token_index + spread * column) % EXPERTS]
        extra = (token_index == (position + 1) % spread) & (column == 0)
        chosen = jnp.where(extra, hot_one, chosen)
        noise = jax.random.randint(ckey, (TOK, TOPK), 0, 1024, dtype=jnp.int32) * TOPK + column
        shuffle = jnp.argsort(noise, axis=1)
        chosen = jnp.take_along_axis(chosen, shuffle, axis=1)
        token_order = jax.random.permutation(tkey, TOK)
        return chosen[token_order]
    drawn = jax.vmap(one_block)(order_keys, token_keys, choice_keys, hot_block)
    return drawn.reshape(SECTIONS, N_EXPERT * TOK, TOPK).astype(jnp.int32)


def shard_levels(rng, dims, cuts, smallest, largest):
    gain, own = 1.0, jax.random.fold_in(rng, 6)
    for dim, blocks in cuts:
        steps = jnp.exp(jax.random.uniform(jax.random.fold_in(own, dim), (blocks,), jnp.float32, smallest / len(cuts), largest / len(cuts)))
        gain = gain * jnp.repeat(steps, dims[dim] // blocks).reshape([-1 if axis == dim else 1 for axis in range(len(dims))])
    return gain


def centred(key, shape, deviation, reach, cuts=(), kind=jnp.bfloat16):
    array = deviation * jax.random.normal(key, shape, jnp.float32)
    if cuts:
        array = array * shard_levels(key, shape, cuts, -0.22, 0.18)
    return jnp.clip(array, -reach, reach).astype(kind)


def setup_inputs(seed: int = 0) -> dict:
    key_list = jax.random.split(jax.random.key(seed), 6)
    sent_grad = centred(key_list[0], (SECTIONS, TOKENS, D), 0.5, 4.0, ((0, 4), (1, 64), (2, 4)))
    head_grad = centred(key_list[1], (TOKENS, D), 0.5, 4.0, ((0, 64), (1, 4)))
    probs = jnp.clip(0.049804688 + 0.9501953 * jax.random.uniform(key_list[2], (SECTIONS, TOKENS, TOPK), jnp.float32) ** shard_levels(key_list[2], (SECTIONS, TOKENS, TOPK), ((0, 4), (1, 64)), -0.2, 0.2), 0.049804688, 1.0).astype(jnp.bfloat16)
    expert_ids = draw_expert_ids(jax.random.fold_in(key_list[5], 71), 0)
    hidden_act = centred(key_list[4], (SECTIONS, EXPERTS, SLOTS, HID), SLOTS ** -0.5, 0.1875, ((0, 4), (1, 64), (3, 4)))
    return dict(sent_grad=sent_grad, head_grad=head_grad, probs=probs, expert_ids=expert_ids, hidden_act=hidden_act)


def reference(sent_grad, head_grad, probs, expert_ids, hidden_act):
    sections = sent_grad.shape[0]
    tokens = sent_grad.shape[1]
    feature_count = sent_grad.shape[2]
    groups = tokens // TOK
    slot_count = groups * MOST
    grad_list = []
    for section in range(sections):
        if section == sections - 1:
            incoming = head_grad
        else:
            incoming = sent_grad[section + 1]
        pair_ids = expert_ids[section].reshape(groups, TOK * TOPK)
        onehot = (pair_ids[:, :, None] == jnp.arange(EXPERTS, dtype=jnp.int32)[None, None, :]).astype(jnp.int32)
        before = jnp.cumsum(onehot, axis=1) - onehot
        slot_rank = jnp.sum(before * onehot, axis=2).astype(jnp.int32)
        block_index = jnp.arange(groups, dtype=jnp.int32)[:, None]
        target = (pair_ids * slot_count + block_index * MOST + slot_rank).reshape(-1).astype(jnp.int32)
        copies = jnp.repeat(incoming, TOPK, axis=0)
        routed = jnp.zeros((EXPERTS * slot_count, feature_count), incoming.dtype).at[target].set(copies)
        routed = routed.reshape(EXPERTS, slot_count, feature_count)
        gate_slots = jnp.zeros((EXPERTS * slot_count,), probs.dtype).at[target].set(probs[section].reshape(-1))
        gate_slots = gate_slots.reshape(EXPERTS, slot_count)

        def expert_step(pieces):
            rows_e, gate_e, act_e = pieces
            weighted = (rows_e.astype(jnp.float32) * gate_e.astype(jnp.float32)[:, None]).astype(jnp.bfloat16)
            return jnp.dot(act_e.T, weighted, preferred_element_type=jnp.float32).astype(jnp.bfloat16)

        weight_grad = lax.map(expert_step, (routed, gate_slots, hidden_act[section]))
        grad_list.append(weight_grad)
    return jnp.stack(grad_list)
```

```python
import jax
import jax.numpy as jnp
from jax import lax
from jax.sharding import PartitionSpec as P

EXPERTS = 64
TOPK = 8
TOK = 128
MOST = 17


def local(sent_grad, head_grad, probs, expert_ids, hidden_act):
    pipes = lax.axis_size("pipe")
    pairs = [(i, i - 1) for i in range(1, pipes)]
    shifted = lax.ppermute(sent_grad, "pipe", pairs)
    is_last = lax.axis_index("pipe") == pipes - 1
    incoming = jnp.where(is_last, head_grad, shifted[0])
    meta = jnp.concatenate([expert_ids[0].T.astype(jnp.bfloat16), probs[0].T], axis=0)
    metas = lax.all_gather(meta, "expert", axis=0)
    tokens = lax.all_gather(incoming, "expert", axis=0)
    me = lax.axis_index("expert").astype(jnp.bfloat16)
    hit = metas[:, :TOPK, :] == me
    gate = jnp.sum(jnp.where(hit, metas[:, TOPK:, :], 0).astype(jnp.float32), axis=1)
    routed = jnp.any(hit, axis=1)
    upper = (jnp.arange(TOK)[:, None] < jnp.arange(TOK)[None, :]).astype(jnp.bfloat16)
    rank = jnp.dot(routed.astype(jnp.bfloat16), upper, preferred_element_type=jnp.float32)
    slot = jnp.where(routed, rank, -1.0).astype(jnp.int32)
    pick = jnp.where(
        slot[:, None, :] == jnp.arange(MOST, dtype=jnp.int32)[None, :, None], gate[:, None, :], 0.0
    ).astype(jnp.bfloat16)
    weighted = jnp.einsum(
        "brn,bnd->brd", pick, tokens, preferred_element_type=jnp.float32
    ).astype(jnp.bfloat16)
    rows = weighted.reshape(EXPERTS * MOST, -1)
    full = lax.all_gather(rows, "tensor", axis=1, tiled=True)
    grad = jnp.einsum("sh,sd->hd", hidden_act[0, 0], full, preferred_element_type=jnp.float32)
    return grad.astype(jnp.bfloat16)[None, None]


def solution(mesh):
    in_specs = (
        P("pipe", "expert", "tensor"),
        P("expert", "tensor"),
        P("pipe", "expert", None),
        P("pipe", "expert", None),
        P("pipe", "expert", None, "tensor"),
    )
    out_specs = P("pipe", "expert", "tensor", None)
    return jax.shard_map(local, mesh=mesh, in_specs=in_specs, out_specs=out_specs, check_vma=False)
```

```python
import functools

import jax
import jax.numpy as jnp
from jax import lax
from jax.experimental import pallas as pl
from jax.experimental.pallas import tpu as pltpu
from jax.sharding import PartitionSpec as P

TOPK = 8
MOST = 17
CHUNKS = 4
MESH = pl.DeviceIdType.MESH


def kernel(
    pipes,
    chips,
    sides,
    meta_ref,
    hidden_ref,
    sent_ref,
    head_ref,
    out_ref,
    tokens,
    metas,
    pick,
    hidden,
    rows,
    acc,
    out_buf,
    own_sem,
    own_send,
    next_send,
    next_recv,
    prev_send,
    prev_recv,
    twin_send,
    twin_recv,
    side_send,
    side_recv,
    out_sem,
):
    tok, feat = sent_ref.shape
    piece = tok // CHUNKS
    half = chips // 2
    units = chips // 4
    block = 8 * tok
    unit_slots = 8 * MOST
    pad_slots = rows.shape[1] // units
    first = (pad_slots // 32) * 16 + (16 if pad_slots % 32 else 0)
    hid = hidden_ref.shape[1]

    me = lax.axis_index("expert")
    pipe = lax.axis_index("pipe")
    side = lax.axis_index("tensor")
    z = me // 2
    core = me % 2
    experts = 2 * chips
    to_next = {"expert": lax.rem(me + 2, experts)}
    to_prev = {"expert": lax.rem(me + experts - 2, experts)}
    to_twin = {"expert": me + 1 - 2 * core}
    to_right = {"tensor": lax.rem(side + 1, sides)}
    to_left = {"tensor": lax.rem(side + sides - 1, sides)}
    to_lower = {"pipe": lax.rem(pipe + pipes - 1, pipes)}
    to_upper = {"pipe": lax.rem(pipe + 1, pipes)}

    def place_up(d):
        return 4 * (d // 2) + d % 2

    def place_down(d):
        return 4 * ((d - 1) // 2) + 2 + (d - 1) % 2

    def part(place, parity, index):
        start = pl.multiple_of((place * 2 + parity) * tok + index * piece, piece)
        return tokens.at[pl.ds(start, piece), :]

    def whole(place, parity):
        return tokens.at[pl.ds(pl.multiple_of((place * 2 + parity) * tok, tok), tok), :]

    def remote(src, dst, send, recv, device):
        return pltpu.make_async_remote_copy(
            src_ref=src,
            dst_ref=dst,
            send_sem=send,
            recv_sem=recv,
            device_id=device,
            device_id_type=MESH,
        )

    def own_local(index):
        span = pl.ds(index * piece, piece)
        return pltpu.make_async_copy(
            head_ref.at[span, :], part(0, core, index), own_sem.at[index]
        )

    def own_remote(index):
        span = pl.ds(index * piece, piece)
        return remote(
            sent_ref.at[span, :],
            part(0, core, index),
            own_send.at[index],
            own_sem.at[index],
            to_lower,
        )

    def ring(send, recv, device, src, dst, step, index):
        if index < CHUNKS:
            a, b = part(src, core, index), part(dst, core, index)
        else:
            a, b = metas.at[src * 2 + core], metas.at[dst * 2 + core]
        return remote(a, b, send.at[step % 2, index], recv.at[step + 1, index], device)

    def next_copy(step, index):
        src = place_down(step) if not isinstance(step, int) or step > 0 else 0
        return ring(next_send, next_recv, to_next, src, place_down(step + 1), step, index)

    def prev_copy(step, index):
        far = place_up(step + 1)
        dst = jnp.where(step + 1 == half, place_down(half), far)
        return ring(prev_send, prev_recv, to_prev, place_up(step), dst, step, index)

    def twin_copies(place, parity, way, slot):
        return (
            remote(
                whole(place, parity),
                whole(place, parity),
                twin_send.at[way, slot, 0],
                twin_recv.at[place, 0],
                to_twin,
            ),
            remote(
                metas.at[place * 2 + parity],
                metas.at[place * 2 + parity],
                twin_send.at[way, slot, 1],
                twin_recv.at[place, 1],
                to_twin,
            ),
        )

    def row_span(unit, start, size):
        return pl.ds(pl.multiple_of(unit * pad_slots + start, 16), size)

    def side_copy(unit, which):
        a = row_span(unit, 0, first)
        b = row_span(unit, first, pad_slots - first)
        src, dst, span, device = (
            (0, 2, a, to_right),
            (0, 2, b, to_right),
            (0, 1, b, to_left),
            (0, 1, a, to_left),
            (2, 3, a, to_right),
            (1, 3, b, to_left),
        )[which]
        return remote(
            rows.at[src, span, :],
            rows.at[dst, span, :],
            side_send.at[unit, which],
            side_recv.at[unit, which],
            device,
        )

    own_meta = pltpu.make_async_copy(meta_ref, metas.at[core], out_sem.at[0])
    own_meta.start()

    @pl.when(pipe == pipes - 1)
    def _():
        for index in range(CHUNKS):
            own_local(index).start()

    barrier = pltpu.get_barrier_semaphore()
    for device in (to_next, to_prev, to_twin, to_right, to_left, to_lower, to_upper):
        pl.semaphore_signal(barrier, inc=1, device_id=device, device_id_type=MESH)
    pl.semaphore_wait(barrier, 7)

    @pl.when(pipe > 0)
    def _():
        for index in range(CHUNKS):
            own_remote(index).start()

    own_meta.wait()
    next_copy(0, CHUNKS).start()
    prev_copy(0, CHUNKS).start()
    for index in range(CHUNKS):

        @pl.when(pipe == pipes - 1)
        def _():
            own_local(index).wait()

        @pl.when(pipe < pipes - 1)
        def _():
            own_remote(index).wait_recv()

        next_copy(0, index).start()
        prev_copy(0, index).start()
    for copy in twin_copies(0, core, 0, 0):
        copy.start()

    slot_iota = lax.broadcasted_iota(jnp.int32, (pad_slots, tok), 0).astype(jnp.float32)
    before = (
        lax.broadcasted_iota(jnp.int32, (tok, tok), 0)
        < lax.broadcasted_iota(jnp.int32, (tok, tok), 1)
    ).astype(jnp.float32)
    mine = me.astype(jnp.float32)

    def unit_places(unit):
        return [4 * unit + q for q in range(4)]

    def prepare(unit):
        for place in unit_places(unit):
            for copy in twin_copies(place, 1 - core, 0, 0):
                copy.wait_recv()
        gates, hits = [], []
        for b in range(8):
            meta = metas[unit * 8 + b].astype(jnp.float32)
            hit = meta[:TOPK] == mine
            gates.append(jnp.sum(jnp.where(hit, meta[TOPK:], 0.0), axis=0, keepdims=True))
            hits.append(jnp.sum(jnp.where(hit, 1.0, 0.0), axis=0, keepdims=True))
        routed = jnp.concatenate(hits, axis=0)
        rank = jnp.dot(routed, before, preferred_element_type=jnp.float32)
        for b in range(8):
            slot = jnp.where(routed[b : b + 1] > 0.5, rank[b : b + 1] + b * MOST, -1.0)
            pick[:, b * tok : (b + 1) * tok] = jnp.where(
                slot_iota == slot, gates[b], 0.0
            ).astype(jnp.bfloat16)
        total = hidden_ref.shape[0]
        i = lax.broadcasted_iota(jnp.int32, (pad_slots, total), 0)
        width = 2 * MOST
        offsets = (2 * unit, 2 * unit + 1, chips - 2 * unit - 1, chips - 2 * unit - 2)
        target = jnp.full((pad_slots, total), -1, jnp.int32)
        for q in range(4):
            chip = lax.rem(z + offsets[q], chips)
            inside = (i >= q * width) & (i < (q + 1) * width)
            target = jnp.where(inside, i + (chip - q) * width, target)
        order = (lax.broadcasted_iota(jnp.int32, (pad_slots, total), 1) == target).astype(
            jnp.bfloat16
        )
        hidden[row_span(unit, 0, pad_slots), :] = jnp.dot(
            order, hidden_ref[...], preferred_element_type=jnp.float32
        ).astype(jnp.bfloat16)

    def select(unit, start, size):
        span = pl.ds(pl.multiple_of(unit * block, block), block)
        rows[0, row_span(unit, 0, pad_slots), start : start + size] = jnp.dot(
            pick[...], tokens[span, start : start + size], preferred_element_type=jnp.float32
        ).astype(jnp.bfloat16)

    def product(which, begin, end):
        span = slice(begin * pad_slots, end * pad_slots)
        return lax.dot_general(
            hidden[span, :],
            rows[which, span, :],
            (((0,), (0,)), ((), ())),
            preferred_element_type=jnp.float32,
        )

    def wait_sides(unit, parts):
        for which in parts:
            side_copy(unit, which).wait_recv()

    def settle(which, begin, end):
        for unit in range(begin, end):
            wait_sides(unit, ((), (3,), (1,), (4, 5))[which])

    def forward(unit):
        wait_sides(unit, (0, 2))
        side_copy(unit, 4).start()
        side_copy(unit, 5).start()

    def arrived(recv, place, step, index):
        if index < CHUNKS:
            a = part(place, core, index)
        else:
            a = metas.at[place * 2 + core]
        remote(a, a, next_send.at[0, index], recv.at[step, index], to_next).wait_recv()

    cut = min(feat, 512)
    early = max(0, (half - 10) // 2 + 1)

    def advance(step, carry):
        odd = lax.rem(step, 2) == 1
        unit = (step - 3) // 2
        busy = odd & (step >= 3)
        down = place_down(step)
        up = place_up(step)
        forward_next = (step < half - 1) | (core == 0)
        forward_prev = (step < half - 1) | (core == 1)
        for index in (CHUNKS, *range(CHUNKS)):
            arrived(next_recv, down, step, index)

            @pl.when(forward_next)
            def _():
                @pl.when(step >= 2)
                def _():
                    next_copy(step, index).wait_send()

                next_copy(step, index).start()

            arrived(prev_recv, up, step, index)

            @pl.when(forward_prev)
            def _():
                @pl.when(step >= 2)
                def _():
                    prev_copy(step, index).wait_send()

                prev_copy(step, index).start()

            if index == 0:

                @pl.when(busy)
                def _():
                    prepare(unit)

            if index == 1:

                @pl.when(busy)
                def _():
                    select(unit, 0, cut)

            if index == 2 and cut < feat:

                @pl.when(busy)
                def _():
                    select(unit, cut, feat - cut)

            if index == 3:

                @pl.when(busy & (unit >= 1))
                def _():
                    forward(unit - 1)

                @pl.when(busy)
                def _():
                    for which in range(4):
                        side_copy(unit, which).start()

            if early and index < CHUNKS:

                @pl.when(step == half - 2)
                def _():
                    settle(index, 0, early)
                    acc[index] = product(index, 0, early)

        @pl.when(step >= 2)
        def _():
            for copy in twin_copies(down, core, 0, step % 2):
                copy.wait_send()

        for copy in twin_copies(down, core, 0, step % 2):
            copy.start()

        @pl.when(step >= 3)
        def _():
            for copy in twin_copies(up, core, 1, step % 2):
                copy.wait_send()

        for copy in twin_copies(up, core, 1, step % 2):
            copy.start()
        return carry

    lax.fori_loop(1, half, advance, 0)

    last = place_down(half)
    for way, recv in ((0, next_recv), (1, prev_recv)):

        @pl.when(core == way)
        def _():
            for index in (CHUNKS, *range(CHUNKS)):
                arrived(recv, last, half, index)
            for copy in twin_copies(last, core, way, half % 2):
                copy.wait_send()
            for copy in twin_copies(last, core, way, half % 2):
                copy.start()

    late = max(early, units - 2)
    if late > early:
        for which in range(4):
            settle(which, early, late)
            more = product(which, early, late)
            acc[which] = acc[which] + more if early else more
    prepare(units - 1)
    select(units - 1, 0, cut)
    if cut < feat:
        select(units - 1, cut, feat - cut)
    for which in range(4):
        side_copy(units - 1, which).start()
    for unit in range(late, units):
        forward(unit)
    for which in range(4):
        settle(which, late, units)
        total = product(which, late, units)
        if late:
            total = total + acc[which]
        out_buf[which] = total.astype(out_buf.dtype)
        owner = lax.rem(side + (0, 1, sides - 1, 2)[which], sides)
        columns = pl.ds(pl.multiple_of(owner * feat, 128), feat)
        pltpu.make_async_copy(out_buf.at[which], out_ref.at[:, columns], out_sem.at[which]).start()

    for index in range(CHUNKS + 1):
        for parity in range(2):
            next_copy(half - 2 + parity, index).wait_send()
            prev_copy(half - 2 + parity, index).wait_send()
    for way in range(2):
        for parity in range(2):
            for copy in twin_copies(0, core, way, parity):
                copy.wait_send()

    def drain(unit, carry):
        for which in range(6):
            side_copy(unit, which).wait_send()
        return carry

    lax.fori_loop(0, units, drain, 0)

    @pl.when(pipe > 0)
    def _():
        for index in range(CHUNKS):
            own_remote(index).wait_send()

    for which in range(4):
        pltpu.make_async_copy(
            out_buf.at[which], out_ref.at[:, pl.ds(0, feat)], out_sem.at[which]
        ).wait()


def local(sent_grad, head_grad, probs, expert_ids, hidden_act):
    pipes = lax.axis_size("pipe")
    experts = lax.axis_size("expert")
    sides = lax.axis_size("tensor")
    chips = experts // 2
    half = chips // 2
    units = chips // 4
    tok, feat = head_grad.shape
    hid = hidden_act.shape[3]
    pad_slots = -(-8 * MOST // 16) * 16
    meta = jnp.concatenate([expert_ids[0].T.astype(jnp.bfloat16), probs[0].T], axis=0)
    bf16 = jnp.bfloat16
    dma = pltpu.SemaphoreType.DMA
    vmem = pl.BlockSpec(memory_space=pltpu.VMEM)
    anywhere = pl.BlockSpec(memory_space=pl.ANY)
    grad = pl.pallas_call(
        functools.partial(kernel, pipes, chips, sides),
        out_shape=jax.ShapeDtypeStruct((hid, sides * feat), bf16),
        in_specs=[vmem, vmem, anywhere, anywhere],
        out_specs=anywhere,
        scratch_shapes=[
            pltpu.VMEM((experts * tok, feat), bf16),
            pltpu.VMEM((experts, 2 * TOPK, tok), bf16),
            pltpu.VMEM((pad_slots, 8 * tok), bf16),
            pltpu.VMEM((units * pad_slots, hid), bf16),
            pltpu.VMEM((4, units * pad_slots, feat), bf16),
            pltpu.VMEM((4, hid, feat), jnp.float32),
            pltpu.VMEM((4, hid, feat), bf16),
            dma((CHUNKS,)),
            dma((CHUNKS,)),
            dma((2, CHUNKS + 1)),
            dma((half + 1, CHUNKS + 1)),
            dma((2, CHUNKS + 1)),
            dma((half + 1, CHUNKS + 1)),
            dma((2, 2, 2)),
            dma((chips, 2)),
            dma((units, 6)),
            dma((units, 6)),
            dma((4,)),
        ],
        compiler_params=pltpu.CompilerParams(
            collective_id=0, has_side_effects=True, vmem_limit_bytes=60_000_000
        ),
    )(meta, hidden_act[0, 0], sent_grad[0], head_grad)
    return grad[None, None]


def solution(mesh):
    in_specs = (
        P("pipe", "expert", "tensor"),
        P("expert", "tensor"),
        P("pipe", "expert", None),
        P("pipe", "expert", None),
        P("pipe", "expert", None, "tensor"),
    )
    out_specs = P("pipe", "expert", "tensor", None)
    return jax.shard_map(local, mesh=mesh, in_specs=in_specs, out_specs=out_specs, check_vma=False)
```

```python
import functools

import jax
import jax.numpy as jnp
from jax import lax
from jax.experimental import pallas as pl
from jax.experimental.pallas import tpu as pltpu
from jax.sharding import PartitionSpec as P

TOPK = 8
MOST = 17
CHUNKS = 4
MESH = pl.DeviceIdType.MESH
SIDE_PARTS = ((), (3,), (1,), (4, 5))


def kernel(
    pipes,
    chips,
    sides,
    ids_ref,
    probs_ref,
    hidden_ref,
    sent_ref,
    head_ref,
    out_ref,
    tokens,
    metas,
    pick_a,
    pick_b,
    ids_in,
    probs_in,
    hidden_in,
    hidden,
    rows,
    acc,
    out_buf,
    own_sem,
    own_send,
    next_send,
    next_recv,
    prev_send,
    prev_recv,
    twin_send,
    twin_recv,
    side_send,
    side_recv,
    out_sem,
):
    tok, feat = sent_ref.shape
    piece = tok // CHUNKS
    half = chips // 2
    units = chips // 4
    block = 8 * tok
    pad_slots = rows.shape[1] // units
    lead = pick_a.shape[0]
    hid = hidden_ref.shape[1]

    me = lax.axis_index("expert")
    pipe = lax.axis_index("pipe")
    side = lax.axis_index("tensor")
    z = me // 2
    core = me % 2
    experts = 2 * chips
    to_next = {"expert": lax.rem(me + 2, experts)}
    to_prev = {"expert": lax.rem(me + experts - 2, experts)}
    to_twin = {"expert": me + 1 - 2 * core}
    turn = 1 - 2 * core
    right = lax.rem(side + sides + turn, sides)
    left = lax.rem(side + sides - turn, sides)
    to_right = {"tensor": right}
    to_left = {"tensor": left}
    to_lower = {"pipe": lax.rem(pipe + pipes - 1, pipes)}
    to_upper = {"pipe": lax.rem(pipe + 1, pipes)}

    def place_up(d):
        return 4 * (d // 2) + d % 2

    def place_down(d):
        return 4 * ((d - 1) // 2) + 2 + (d - 1) % 2

    def part(place, parity, index):
        start = pl.multiple_of((place * 2 + parity) * tok + index * piece, piece)
        return tokens.at[pl.ds(start, piece), :]

    def whole(place, parity):
        return tokens.at[pl.ds(pl.multiple_of((place * 2 + parity) * tok, tok), tok), :]

    def remote(src, dst, send, recv, device):
        return pltpu.make_async_remote_copy(
            src_ref=src,
            dst_ref=dst,
            send_sem=send,
            recv_sem=recv,
            device_id=device,
            device_id_type=MESH,
        )

    def own_local(index):
        span = pl.ds(index * piece, piece)
        return pltpu.make_async_copy(
            head_ref.at[span, :], part(0, core, index), own_sem.at[index]
        )

    def own_remote(index):
        span = pl.ds(index * piece, piece)
        return remote(
            sent_ref.at[span, :],
            part(0, core, index),
            own_send.at[index],
            own_sem.at[index],
            to_lower,
        )

    def ring(send, recv, device, src, dst, step, index):
        if index < CHUNKS:
            a, b = part(src, core, index), part(dst, core, index)
        else:
            a, b = metas.at[src * 2 + core], metas.at[dst * 2 + core]
        return remote(a, b, send.at[step % 2, index], recv.at[step + 1, index], device)

    def next_copy(step, index):
        src = place_down(step) if not isinstance(step, int) or step > 0 else 0
        return ring(next_send, next_recv, to_next, src, place_down(step + 1), step, index)

    def prev_copy(step, index):
        far = place_up(step + 1)
        dst = jnp.where(step + 1 == half, place_down(half), far)
        return ring(prev_send, prev_recv, to_prev, place_up(step), dst, step, index)

    def twin_copies(place, parity, way, slot):
        return (
            remote(
                whole(place, parity),
                whole(place, parity),
                twin_send.at[way, slot, 0],
                twin_recv.at[place, 0],
                to_twin,
            ),
            remote(
                metas.at[place * 2 + parity],
                metas.at[place * 2 + parity],
                twin_send.at[way, slot, 1],
                twin_recv.at[place, 1],
                to_twin,
            ),
        )

    def row_span(unit, start, size):
        return pl.ds(pl.multiple_of(unit * pad_slots + start, 16), size)

    def side_copy(unit, kind, which):
        if kind == 0:
            cut_a, cut_b = (0, lead // 2), (lead // 2, lead // 2)
        else:
            rest = pad_slots - lead
            size = (rest // 32) * 16 + (16 if rest % 32 else 0)
            cut_a, cut_b = (lead, size), (lead + size, rest - size)
        a, b = row_span(unit, *cut_a), row_span(unit, *cut_b)
        src, dst, span, device = (
            (0, 2, a, to_right),
            (0, 2, b, to_right),
            (0, 1, b, to_left),
            (0, 1, a, to_left),
            (2, 3, a, to_right),
            (1, 3, b, to_left),
        )[which]
        return remote(
            rows.at[src, span, :],
            rows.at[dst, span, :],
            side_send.at[unit, kind, which],
            side_recv.at[unit, kind, which],
            device,
        )

    own_ids = pltpu.make_async_copy(ids_ref, ids_in, out_sem.at[1])
    own_probs = pltpu.make_async_copy(probs_ref, probs_in, out_sem.at[2])
    own_hidden = pltpu.make_async_copy(hidden_ref, hidden_in, out_sem.at[0])
    own_ids.start()
    own_probs.start()
    own_hidden.start()
    own_ids.wait()
    own_probs.wait()
    metas[core] = jnp.concatenate(
        [ids_in[...].astype(jnp.float32), probs_in[...].astype(jnp.float32)], axis=0
    ).astype(metas.dtype)

    @pl.when(pipe == pipes - 1)
    def _():
        for index in range(CHUNKS):
            own_local(index).start()

    barrier = pltpu.get_barrier_semaphore()
    for device in (to_next, to_prev, to_twin, to_right, to_left, to_lower, to_upper):
        pl.semaphore_signal(barrier, inc=1, device_id=device, device_id_type=MESH)
    pl.semaphore_wait(barrier, 7)

    @pl.when(pipe > 0)
    def _():
        for index in range(CHUNKS):
            own_remote(index).start()

    next_copy(0, CHUNKS).start()
    prev_copy(0, CHUNKS).start()
    for index in range(CHUNKS):

        @pl.when(pipe == pipes - 1)
        def _():
            own_local(index).wait()

        @pl.when(pipe < pipes - 1)
        def _():
            own_remote(index).wait_recv()

        next_copy(0, index).start()
        prev_copy(0, index).start()
    for copy in twin_copies(0, core, 0, 0):
        copy.start()
    own_hidden.wait()

    before = (
        lax.broadcasted_iota(jnp.int32, (tok, tok), 0)
        < lax.broadcasted_iota(jnp.int32, (tok, tok), 1)
    ).astype(jnp.float32)
    mine = me.astype(jnp.float32)

    def twin_wait(unit, quarters):
        for q in quarters:
            for copy in twin_copies(4 * unit + q, 1 - core, 0, 0):
                copy.wait_recv()

    def mark(pick, unit, blocks, base):
        gates, hits = [], []
        for b in blocks:
            meta = metas[unit * 8 + b].astype(jnp.float32)
            hit = meta[:TOPK] == mine
            gates.append(jnp.sum(jnp.where(hit, meta[TOPK:], 0.0), axis=0, keepdims=True))
            hits.append(jnp.sum(jnp.where(hit, 1.0, 0.0), axis=0, keepdims=True))
        spare = jnp.zeros((8 - len(blocks), tok), jnp.float32)
        routed = jnp.concatenate([*hits, spare], axis=0)
        rank = jnp.dot(routed, before, preferred_element_type=jnp.float32)
        slots = (
            lax.broadcasted_iota(jnp.int32, (pick.shape[0], tok), 0) + base
        ).astype(jnp.float32)
        for n, b in enumerate(blocks):
            slot = jnp.where(routed[n : n + 1] > 0.5, rank[n : n + 1] + b * MOST, -1.0)
            pick[:, n * tok : (n + 1) * tok] = jnp.where(slots == slot, gates[n], 0.0).astype(
                pick.dtype
            )

    def prepare_a(unit):
        twin_wait(unit, (0, 1, 2))
        mark(pick_a, unit, range(6), 0)
        total = hidden_in.shape[0]
        i = lax.broadcasted_iota(jnp.int32, (pad_slots, total), 0)
        width = 2 * MOST
        offsets = (2 * unit, 2 * unit + 1, chips - 2 * unit - 1, chips - 2 * unit - 2)
        target = jnp.full((pad_slots, total), -1, jnp.int32)
        for q in range(4):
            chip = lax.rem(z + offsets[q], chips)
            inside = (i >= q * width) & (i < (q + 1) * width)
            target = jnp.where(inside, i + (chip - q) * width, target)
        order = (lax.broadcasted_iota(jnp.int32, (pad_slots, total), 1) == target).astype(
            jnp.bfloat16
        )
        hidden[row_span(unit, 0, pad_slots), :] = jnp.dot(
            order, hidden_in[...], preferred_element_type=jnp.float32
        ).astype(jnp.bfloat16)

    def prepare_b(unit):
        twin_wait(unit, (3,))
        mark(pick_b, unit, range(5, 8), lead)

    def select(unit, kind, start, size):
        pick, base, skip = ((pick_a, 0, 0), (pick_b, lead, 5 * tok))[kind]
        span = pl.ds(pl.multiple_of(unit * block + skip, tok), pick.shape[1])
        rows[0, row_span(unit, base, pick.shape[0]), start : start + size] = jnp.dot(
            pick[...], tokens[span, start : start + size], preferred_element_type=jnp.float32
        ).astype(jnp.bfloat16)

    def send(unit, kind):
        for which in range(4):
            side_copy(unit, kind, which).start()

    def product(which, begin, end):
        span = slice(begin, end)
        return lax.dot_general(
            hidden[span, :],
            rows[which, span, :],
            (((0,), (0,)), ((), ())),
            preferred_element_type=jnp.float32,
        )

    def wait_sides(unit, kind, parts):
        for which in parts:
            side_copy(unit, kind, which).wait_recv()

    def settle(which, begin, end):
        for unit in range(begin, end):
            for kind in range(2):
                wait_sides(unit, kind, SIDE_PARTS[which])

    def forward(unit, kind):
        wait_sides(unit, kind, (0, 2))
        side_copy(unit, kind, 4).start()
        side_copy(unit, kind, 5).start()

    def arrived(recv, place, step, index):
        if index < CHUNKS:
            a = part(place, core, index)
        else:
            a = metas.at[place * 2 + core]
        remote(a, a, next_send.at[0, index], recv.at[step, index], to_next).wait_recv()

    cut = min(feat, 512)
    early = max(0, (half - 9) // 2 + 1)
    wide = cut < feat

    def advance(step, carry):
        even = lax.rem(step, 2) == 0
        unit_a = (step - 2) // 2
        unit_b = (step - 3) // 2
        busy_a = even & (step >= 2)
        busy_b = (lax.rem(step, 2) == 1) & (step >= 3)
        down = place_down(step)
        up = place_up(step)
        forward_next = (step < half - 1) | (core == 0)
        forward_prev = (step < half - 1) | (core == 1)
        for index in (CHUNKS, *range(CHUNKS)):
            arrived(next_recv, down, step, index)

            @pl.when(forward_next)
            def _():
                @pl.when(step >= 2)
                def _():
                    next_copy(step, index).wait_send()

                next_copy(step, index).start()

            arrived(prev_recv, up, step, index)

            @pl.when(forward_prev)
            def _():
                @pl.when(step >= 2)
                def _():
                    prev_copy(step, index).wait_send()

                prev_copy(step, index).start()

            if index == 0:

                @pl.when(busy_a & (step >= 4))
                def _():
                    forward(unit_a - 1, 0)

                @pl.when(busy_a)
                def _():
                    prepare_a(unit_a)

                @pl.when(busy_b & (step >= 5))
                def _():
                    forward(unit_b - 1, 1)

                @pl.when(busy_b)
                def _():
                    prepare_b(unit_b)

            for kind, busy, unit in ((0, busy_a, unit_a), (1, busy_b, unit_b)):
                if index == 1:

                    @pl.when(busy)
                    def _():
                        select(unit, kind, 0, cut)

                if index == 2:

                    @pl.when(busy)
                    def _():
                        if wide:
                            select(unit, kind, cut, feat - cut)
                        send(unit, kind)

            if early and index < 4:

                @pl.when(step == half - 2)
                def _():
                    settle(index, 0, early)
                    acc[index] = product(index, 0, early * pad_slots)

        @pl.when(step >= 2)
        def _():
            for copy in twin_copies(down, core, 0, step % 2):
                copy.wait_send()

        for copy in twin_copies(down, core, 0, step % 2):
            copy.start()

        @pl.when(step >= 3)
        def _():
            for copy in twin_copies(up, core, 1, step % 2):
                copy.wait_send()

        for copy in twin_copies(up, core, 1, step % 2):
            copy.start()
        return carry

    lax.fori_loop(1, half, advance, 0)

    def finish(unit, kind):
        (prepare_a, prepare_b)[kind](unit)
        select(unit, kind, 0, cut)
        if wide:
            select(unit, kind, cut, feat - cut)
        send(unit, kind)

    if units > 1:
        forward(units - 2, 0)
    finish(units - 1, 0)

    last = place_down(half)
    for way, recv in ((0, next_recv), (1, prev_recv)):

        @pl.when(core == way)
        def _():
            for index in (CHUNKS, *range(CHUNKS)):
                arrived(recv, last, half, index)
            for copy in twin_copies(last, core, way, half % 2):
                copy.wait_send()
            for copy in twin_copies(last, core, way, half % 2):
                copy.start()

    late = max(early, units - 2)
    split = (units - 1) * pad_slots + lead
    if units > 1:
        forward(units - 2, 1)
    if late > early:
        for which in range(4):
            settle(which, early, late)
            more = product(which, early * pad_slots, late * pad_slots)
            acc[which] = acc[which] + more if early else more
    finish(units - 1, 1)

    def gather_up(which):
        settle(which, late, units - 1)
        wait_sides(units - 1, 0, SIDE_PARTS[which])
        more = product(which, late * pad_slots, split)
        acc[which] = acc[which] + more if late else more

    forward(units - 1, 0)
    for which in range(3):
        gather_up(which)
    forward(units - 1, 1)
    gather_up(3)
    for which in range(4):
        wait_sides(units - 1, 1, SIDE_PARTS[which])
        total = acc[which] + product(which, split, units * pad_slots)
        out_buf[which] = total.astype(out_buf.dtype)
        owner = (side, right, left, lax.rem(side + 2, sides))[which]
        columns = pl.ds(pl.multiple_of(owner * feat, 128), feat)
        pltpu.make_async_copy(out_buf.at[which], out_ref.at[:, columns], out_sem.at[which]).start()

    for index in range(CHUNKS + 1):
        for parity in range(2):
            next_copy(half - 2 + parity, index).wait_send()
            prev_copy(half - 2 + parity, index).wait_send()
    for way in range(2):
        for parity in range(2):
            for copy in twin_copies(0, core, way, parity):
                copy.wait_send()

    def drain(unit, carry):
        for kind in range(2):
            for which in range(6):
                side_copy(unit, kind, which).wait_send()
        return carry

    lax.fori_loop(0, units, drain, 0)

    @pl.when(pipe > 0)
    def _():
        for index in range(CHUNKS):
            own_remote(index).wait_send()

    for which in range(4):
        pltpu.make_async_copy(
            out_buf.at[which], out_ref.at[:, pl.ds(0, feat)], out_sem.at[which]
        ).wait()


def local(sent_grad, head_grad, probs, expert_ids, hidden_act):
    pipes = lax.axis_size("pipe")
    experts = lax.axis_size("expert")
    sides = lax.axis_size("tensor")
    chips = experts // 2
    half = chips // 2
    units = chips // 4
    tok, feat = head_grad.shape
    hid = hidden_act.shape[3]
    pad_slots = -(-8 * MOST // 16) * 16
    lead = 96
    bf16 = jnp.bfloat16
    dma = pltpu.SemaphoreType.DMA
    vmem = pl.BlockSpec(memory_space=pltpu.VMEM)
    anywhere = pl.BlockSpec(memory_space=pl.ANY)
    hbm = pl.BlockSpec(memory_space=pltpu.HBM)
    grad = pl.pallas_call(
        functools.partial(kernel, pipes, chips, sides),
        out_shape=jax.ShapeDtypeStruct((hid, sides * feat), bf16),
        in_specs=[hbm, hbm, hbm, hbm, hbm],
        out_specs=anywhere,
        scratch_shapes=[
            pltpu.VMEM((experts * tok, feat), bf16),
            pltpu.VMEM((experts, 2 * TOPK, tok), bf16),
            pltpu.VMEM((lead, 6 * tok), bf16),
            pltpu.VMEM((pad_slots - lead, 3 * tok), bf16),
            pltpu.VMEM((TOPK, tok), jnp.int32),
            pltpu.VMEM((TOPK, tok), bf16),
            pltpu.VMEM(hidden_act.shape[2:], bf16),
            pltpu.VMEM((units * pad_slots, hid), bf16),
            pltpu.VMEM((4, units * pad_slots, feat), bf16),
            pltpu.VMEM((4, hid, feat), jnp.float32),
            pltpu.VMEM((4, hid, feat), bf16),
            dma((CHUNKS,)),
            dma((CHUNKS,)),
            dma((2, CHUNKS + 1)),
            dma((half + 1, CHUNKS + 1)),
            dma((2, CHUNKS + 1)),
            dma((half + 1, CHUNKS + 1)),
            dma((2, 2, 2)),
            dma((chips, 2)),
            dma((units, 2, 6)),
            dma((units, 2, 6)),
            dma((4,)),
        ],
        compiler_params=pltpu.CompilerParams(
            collective_id=0, has_side_effects=True, vmem_limit_bytes=36_000_000
        ),
    )(*(pltpu.with_memory_space_constraint(a, pltpu.HBM) for a in (expert_ids[0].T, probs[0].T, hidden_act[0, 0], sent_grad[0], head_grad)))
    return grad[None, None]


def solution(mesh):
    in_specs = (
        P("pipe", "expert", "tensor"),
        P("expert", "tensor"),
        P("pipe", "expert", None),
        P("pipe", "expert", None),
        P("pipe", "expert", None, "tensor"),
    )
    out_specs = P("pipe", "expert", "tensor", None)
    return jax.shard_map(local, mesh=mesh, in_specs=in_specs, out_specs=out_specs, check_vma=False)
```

```python
import functools

import jax
import jax.numpy as jnp
from jax import lax
from jax.experimental import pallas as pl
from jax.experimental.pallas import tpu as pltpu
from jax.sharding import PartitionSpec as P

TOPK = 8
MOST = 17
CHUNKS = 4
MESH = pl.DeviceIdType.MESH
SIDE_PARTS = ((), (3,), (1,), (4, 5))


def kernel(
    pipes,
    chips,
    sides,
    ids_ref,
    probs_ref,
    hidden_ref,
    sent_ref,
    head_ref,
    out_ref,
    tokens,
    metas,
    pick_a,
    pick_b,
    pick_c,
    ids_in,
    probs_in,
    hidden_in,
    hidden,
    rows,
    acc,
    out_buf,
    own_sem,
    own_send,
    next_send,
    next_recv,
    prev_send,
    prev_recv,
    twin_send,
    twin_recv,
    side_send,
    side_recv,
    out_sem,
):
    tok, feat = sent_ref.shape
    piece = tok // CHUNKS
    half = chips // 2
    units = chips // 4
    block = 8 * tok
    pad_slots = rows.shape[1] // units
    starts = (0, pick_a.shape[0], pick_a.shape[0] + pick_b.shape[0], pad_slots)
    hid = hidden_ref.shape[1]

    me = lax.axis_index("expert")
    pipe = lax.axis_index("pipe")
    side = lax.axis_index("tensor")
    z = me // 2
    core = me % 2
    experts = 2 * chips
    to_next = {"expert": lax.rem(me + 2, experts)}
    to_prev = {"expert": lax.rem(me + experts - 2, experts)}
    to_twin = {"expert": me + 1 - 2 * core}
    turn = 1 - 2 * core
    right = lax.rem(side + sides + turn, sides)
    left = lax.rem(side + sides - turn, sides)
    to_right = {"tensor": right}
    to_left = {"tensor": left}
    to_lower = {"pipe": lax.rem(pipe + pipes - 1, pipes)}
    to_upper = {"pipe": lax.rem(pipe + 1, pipes)}

    def place_up(d):
        return 4 * (d // 2) + d % 2

    def place_down(d):
        return 4 * ((d - 1) // 2) + 2 + (d - 1) % 2

    def part(place, parity, index):
        start = pl.multiple_of((place * 2 + parity) * tok + index * piece, piece)
        return tokens.at[pl.ds(start, piece), :]

    def whole(place, parity):
        return tokens.at[pl.ds(pl.multiple_of((place * 2 + parity) * tok, tok), tok), :]

    def remote(src, dst, send, recv, device):
        return pltpu.make_async_remote_copy(
            src_ref=src,
            dst_ref=dst,
            send_sem=send,
            recv_sem=recv,
            device_id=device,
            device_id_type=MESH,
        )

    def own_local(index):
        span = pl.ds(index * piece, piece)
        return pltpu.make_async_copy(
            head_ref.at[span, :], part(0, core, index), own_sem.at[index]
        )

    def own_remote(index):
        span = pl.ds(index * piece, piece)
        return remote(
            sent_ref.at[span, :],
            part(0, core, index),
            own_send.at[index],
            own_sem.at[index],
            to_lower,
        )

    def ring(send, recv, device, src, dst, step, index):
        if index < CHUNKS:
            a, b = part(src, core, index), part(dst, core, index)
        else:
            a, b = metas.at[src * 2 + core], metas.at[dst * 2 + core]
        return remote(a, b, send.at[step % 2, index], recv.at[step + 1, index], device)

    def next_copy(step, index):
        src = place_down(step) if not isinstance(step, int) or step > 0 else 0
        return ring(next_send, next_recv, to_next, src, place_down(step + 1), step, index)

    def prev_copy(step, index):
        far = place_up(step + 1)
        dst = jnp.where(step + 1 == half, place_down(half), far)
        return ring(prev_send, prev_recv, to_prev, place_up(step), dst, step, index)

    def twin_copies(place, parity, way, slot):
        return (
            remote(
                whole(place, parity),
                whole(place, parity),
                twin_send.at[way, slot, 0],
                twin_recv.at[place, 0],
                to_twin,
            ),
            remote(
                metas.at[place * 2 + parity],
                metas.at[place * 2 + parity],
                twin_send.at[way, slot, 1],
                twin_recv.at[place, 1],
                to_twin,
            ),
        )

    def row_span(unit, start, size):
        return pl.ds(pl.multiple_of(unit * pad_slots + start, 16), size)

    def side_copy(unit, kind, which):
        size = starts[kind + 1] - starts[kind]
        fore = -(-size // 32) * 16
        cut_a, cut_b = (starts[kind], fore), (starts[kind] + fore, size - fore)
        a, b = row_span(unit, *cut_a), row_span(unit, *cut_b)
        src, dst, span, device = (
            (0, 2, a, to_right),
            (0, 2, b, to_right),
            (0, 1, b, to_left),
            (0, 1, a, to_left),
            (2, 3, a, to_right),
            (1, 3, b, to_left),
        )[which]
        return remote(
            rows.at[src, span, :],
            rows.at[dst, span, :],
            side_send.at[unit, kind, which],
            side_recv.at[unit, kind, which],
            device,
        )

    own_ids = pltpu.make_async_copy(ids_ref, ids_in, out_sem.at[1])
    own_probs = pltpu.make_async_copy(probs_ref, probs_in, out_sem.at[2])
    own_hidden = pltpu.make_async_copy(hidden_ref, hidden_in, out_sem.at[0])
    own_ids.start()
    own_probs.start()
    own_hidden.start()
    own_ids.wait()
    own_probs.wait()
    metas[core] = jnp.concatenate(
        [ids_in[...].astype(jnp.float32), probs_in[...].astype(jnp.float32)], axis=0
    ).astype(metas.dtype)

    @pl.when(pipe == pipes - 1)
    def _():
        for index in range(CHUNKS):
            own_local(index).start()

    barrier = pltpu.get_barrier_semaphore()
    for device in (to_next, to_prev, to_twin, to_right, to_left, to_lower, to_upper):
        pl.semaphore_signal(barrier, inc=1, device_id=device, device_id_type=MESH)
    pl.semaphore_wait(barrier, 7)

    @pl.when(pipe > 0)
    def _():
        for index in range(CHUNKS):
            own_remote(index).start()

    next_copy(0, CHUNKS).start()
    prev_copy(0, CHUNKS).start()
    for index in range(CHUNKS):

        @pl.when(pipe == pipes - 1)
        def _():
            own_local(index).wait()

        @pl.when(pipe < pipes - 1)
        def _():
            own_remote(index).wait_recv()

        next_copy(0, index).start()
        prev_copy(0, index).start()
    for copy in twin_copies(0, core, 0, 0):
        copy.start()
    own_hidden.wait()

    before = (
        lax.broadcasted_iota(jnp.int32, (tok, tok), 0)
        < lax.broadcasted_iota(jnp.int32, (tok, tok), 1)
    ).astype(jnp.float32)
    mine = me.astype(jnp.float32)

    def twin_wait(unit, quarters):
        for q in quarters:
            for copy in twin_copies(4 * unit + q, 1 - core, 0, 0):
                copy.wait_recv()

    def mark(pick, unit, blocks, base):
        gates, hits = [], []
        for b in blocks:
            meta = metas[unit * 8 + b].astype(jnp.float32)
            hit = meta[:TOPK] == mine
            gates.append(jnp.sum(jnp.where(hit, meta[TOPK:], 0.0), axis=0, keepdims=True))
            hits.append(jnp.sum(jnp.where(hit, 1.0, 0.0), axis=0, keepdims=True))
        spare = jnp.zeros((8 - len(blocks), tok), jnp.float32)
        routed = jnp.concatenate([*hits, spare], axis=0)
        rank = jnp.dot(routed, before, preferred_element_type=jnp.float32)
        slots = (
            lax.broadcasted_iota(jnp.int32, (pick.shape[0], tok), 0) + base
        ).astype(jnp.float32)
        for n, b in enumerate(blocks):
            slot = jnp.where(routed[n : n + 1] > 0.5, rank[n : n + 1] + b * MOST, -1.0)
            pick[:, n * tok : (n + 1) * tok] = jnp.where(slots == slot, gates[n], 0.0).astype(
                pick.dtype
            )

    def permute(unit):
        total = hidden_in.shape[0]
        i = lax.broadcasted_iota(jnp.int32, (pad_slots, total), 0)
        width = 2 * MOST
        offsets = (2 * unit, 2 * unit + 1, chips - 2 * unit - 1, chips - 2 * unit - 2)
        target = jnp.full((pad_slots, total), -1, jnp.int32)
        for q in range(4):
            chip = lax.rem(z + offsets[q], chips)
            inside = (i >= q * width) & (i < (q + 1) * width)
            target = jnp.where(inside, i + (chip - q) * width, target)
        order = (lax.broadcasted_iota(jnp.int32, (pad_slots, total), 1) == target).astype(
            jnp.bfloat16
        )
        hidden[row_span(unit, 0, pad_slots), :] = jnp.dot(
            order, hidden_in[...], preferred_element_type=jnp.float32
        ).astype(jnp.bfloat16)

    def prepare_b(unit):
        twin_wait(unit, (3,))
        mark(pick_b, unit, range(5, 8), lead)

    parts = (((0,), range(0, 2), pick_a), ((1, 2), range(1, 6), pick_b), ((3,), range(5, 8), pick_c))

    def prepare(unit, kind):
        quarters, blocks, pick = parts[kind]
        twin_wait(unit, quarters)
        mark(pick, unit, blocks, starts[kind])

    def select(unit, kind, start, size):
        pick = parts[kind][2]
        span = pl.ds(pl.multiple_of(unit * block + parts[kind][1][0] * tok, tok), pick.shape[1])
        rows[0, row_span(unit, starts[kind], pick.shape[0]), start : start + size] = jnp.dot(
            pick[...], tokens[span, start : start + size], preferred_element_type=jnp.float32
        ).astype(jnp.bfloat16)

    def send(unit, kind):
        for which in range(4):
            side_copy(unit, kind, which).start()

    def product(which, begin, end):
        span = slice(begin, end)
        return lax.dot_general(
            hidden[span, :],
            rows[which, span, :],
            (((0,), (0,)), ((), ())),
            preferred_element_type=jnp.float32,
        )

    def wait_sides(unit, kind, parts):
        for which in parts:
            side_copy(unit, kind, which).wait_recv()

    def settle(which, begin, end):
        for unit in range(begin, end):
            for kind in range(3):
                wait_sides(unit, kind, SIDE_PARTS[which])

    def forward(unit, kind):
        wait_sides(unit, kind, (0, 2))
        side_copy(unit, kind, 4).start()
        side_copy(unit, kind, 5).start()

    def arrived(recv, place, step, index):
        if index < CHUNKS:
            a = part(place, core, index)
        else:
            a = metas.at[place * 2 + core]
        remote(a, a, next_send.at[0, index], recv.at[step, index], to_next).wait_recv()

    cut = min(feat, 512)
    early = max(0, (half - 9) // 2 + 1)
    wide = cut < feat

    def advance(step, carry):
        even = lax.rem(step, 2) == 0
        odd = lax.rem(step, 2) == 1
        unit_a = (step - 1) // 2
        unit_b = (step - 2) // 2
        unit_c = (step - 3) // 2
        work = ((odd, unit_a), (even, unit_b), (odd & (step >= 3), unit_c))
        down = place_down(step)
        up = place_up(step)
        forward_next = (step < half - 1) | (core == 0)
        forward_prev = (step < half - 1) | (core == 1)
        for index in (CHUNKS, *range(CHUNKS)):
            arrived(next_recv, down, step, index)

            @pl.when(forward_next)
            def _():
                @pl.when(step >= 2)
                def _():
                    next_copy(step, index).wait_send()

                next_copy(step, index).start()

            arrived(prev_recv, up, step, index)

            @pl.when(forward_prev)
            def _():
                @pl.when(step >= 2)
                def _():
                    prev_copy(step, index).wait_send()

                prev_copy(step, index).start()

            for kind, (busy, unit) in enumerate(work):
                if index == 0:

                    @pl.when(busy)
                    def _():
                        prepare(unit, kind)

                        if kind == 1:
                            permute(unit)

                if index == 1:

                    @pl.when(busy)
                    def _():
                        select(unit, kind, 0, cut)

                if index == 2:

                    @pl.when(busy)
                    def _():
                        if wide:
                            select(unit, kind, cut, feat - cut)
                        send(unit, kind)

            if index == 3:

                @pl.when(even)
                def _():
                    forward(unit_b, 0)

                @pl.when(even & (step >= 4))
                def _():
                    forward(unit_b - 1, 2)

                @pl.when(odd & (step >= 3))
                def _():
                    forward(unit_c, 1)

            if early and index < 4:

                @pl.when(step == half - 2)
                def _():
                    settle(index, 0, early)
                    acc[index] = product(index, 0, early * pad_slots)

        @pl.when(step >= 2)
        def _():
            for copy in twin_copies(down, core, 0, step % 2):
                copy.wait_send()

        for copy in twin_copies(down, core, 0, step % 2):
            copy.start()

        @pl.when(step >= 3)
        def _():
            for copy in twin_copies(up, core, 1, step % 2):
                copy.wait_send()

        for copy in twin_copies(up, core, 1, step % 2):
            copy.start()
        return carry

    lax.fori_loop(1, half, advance, 0)

    def finish(unit, kind):
        prepare(unit, kind)
        select(unit, kind, 0, cut)
        if wide:
            select(unit, kind, cut, feat - cut)
        send(unit, kind)

    finish(units - 1, 1)

    last = place_down(half)
    for way, recv in ((0, next_recv), (1, prev_recv)):

        @pl.when(core == way)
        def _():
            for index in (CHUNKS, *range(CHUNKS)):
                arrived(recv, last, half, index)
            for copy in twin_copies(last, core, way, half % 2):
                copy.wait_send()
            for copy in twin_copies(last, core, way, half % 2):
                copy.start()

    late = max(early, units - 2)
    split = (units - 1) * pad_slots + starts[2]
    forward(units - 1, 0)
    if units > 1:
        forward(units - 2, 2)
    permute(units - 1)
    if late > early:
        for which in range(4):
            settle(which, early, late)
            more = product(which, early * pad_slots, late * pad_slots)
            acc[which] = acc[which] + more if early else more
    finish(units - 1, 2)

    def gather_up(which):
        settle(which, late, units - 1)
        wait_sides(units - 1, 0, SIDE_PARTS[which])
        wait_sides(units - 1, 1, SIDE_PARTS[which])
        more = product(which, late * pad_slots, split)
        acc[which] = acc[which] + more if late else more

    forward(units - 1, 1)
    for which in range(3):
        gather_up(which)
    forward(units - 1, 2)
    gather_up(3)
    for which in range(4):
        wait_sides(units - 1, 2, SIDE_PARTS[which])
        total = acc[which] + product(which, split, units * pad_slots)
        out_buf[which] = total.astype(out_buf.dtype)
        owner = (side, right, left, lax.rem(side + 2, sides))[which]
        columns = pl.ds(pl.multiple_of(owner * feat, 128), feat)
        pltpu.make_async_copy(out_buf.at[which], out_ref.at[:, columns], out_sem.at[which]).start()

    for index in range(CHUNKS + 1):
        for parity in range(2):
            next_copy(half - 2 + parity, index).wait_send()
            prev_copy(half - 2 + parity, index).wait_send()
    for way in range(2):
        for parity in range(2):
            for copy in twin_copies(0, core, way, parity):
                copy.wait_send()

    def drain(unit, carry):
        for kind in range(3):
            for which in range(6):
                side_copy(unit, kind, which).wait_send()
        return carry

    lax.fori_loop(0, units, drain, 0)

    @pl.when(pipe > 0)
    def _():
        for index in range(CHUNKS):
            own_remote(index).wait_send()

    for which in range(4):
        pltpu.make_async_copy(
            out_buf.at[which], out_ref.at[:, pl.ds(0, feat)], out_sem.at[which]
        ).wait()


def local(sent_grad, head_grad, probs, expert_ids, hidden_act):
    pipes = lax.axis_size("pipe")
    experts = lax.axis_size("expert")
    sides = lax.axis_size("tensor")
    chips = experts // 2
    half = chips // 2
    units = chips // 4
    tok, feat = head_grad.shape
    hid = hidden_act.shape[3]
    pad_slots = -(-8 * MOST // 16) * 16
    bf16 = jnp.bfloat16
    dma = pltpu.SemaphoreType.DMA
    vmem = pl.BlockSpec(memory_space=pltpu.VMEM)
    anywhere = pl.BlockSpec(memory_space=pl.ANY)
    hbm = pl.BlockSpec(memory_space=pltpu.HBM)
    grad = pl.pallas_call(
        functools.partial(kernel, pipes, chips, sides),
        out_shape=jax.ShapeDtypeStruct((hid, sides * feat), bf16),
        in_specs=[hbm, hbm, hbm, hbm, hbm],
        out_specs=anywhere,
        scratch_shapes=[
            pltpu.VMEM((experts * tok, feat), bf16),
            pltpu.VMEM((experts, 2 * TOPK, tok), bf16),
            pltpu.VMEM((32, 2 * tok), bf16),
            pltpu.VMEM((64, 5 * tok), bf16),
            pltpu.VMEM((pad_slots - 96, 3 * tok), bf16),
            pltpu.VMEM((TOPK, tok), jnp.int32),
            pltpu.VMEM((TOPK, tok), bf16),
            pltpu.VMEM(hidden_act.shape[2:], bf16),
            pltpu.VMEM((units * pad_slots, hid), bf16),
            pltpu.VMEM((4, units * pad_slots, feat), bf16),
            pltpu.VMEM((4, hid, feat), jnp.float32),
            pltpu.VMEM((4, hid, feat), bf16),
            dma((CHUNKS,)),
            dma((CHUNKS,)),
            dma((2, CHUNKS + 1)),
            dma((half + 1, CHUNKS + 1)),
            dma((2, CHUNKS + 1)),
            dma((half + 1, CHUNKS + 1)),
            dma((2, 2, 2)),
            dma((chips, 2)),
            dma((units, 3, 6)),
            dma((units, 3, 6)),
            dma((4,)),
        ],
        compiler_params=pltpu.CompilerParams(
            collective_id=0, has_side_effects=True, vmem_limit_bytes=36_000_000
        ),
    )(*(pltpu.with_memory_space_constraint(a, pltpu.HBM) for a in (expert_ids[0].T, probs[0].T, hidden_act[0, 0], sent_grad[0], head_grad)))
    return grad[None, None]


def solution(mesh):
    in_specs = (
        P("pipe", "expert", "tensor"),
        P("expert", "tensor"),
        P("pipe", "expert", None),
        P("pipe", "expert", None),
        P("pipe", "expert", None, "tensor"),
    )
    out_specs = P("pipe", "expert", "tensor", None)
    return jax.shard_map(local, mesh=mesh, in_specs=in_specs, out_specs=out_specs, check_vma=False)
```

```python
import functools

import jax
import jax.numpy as jnp
from jax import lax
from jax.experimental import pallas as pl
from jax.experimental.pallas import tpu as pltpu
from jax.sharding import PartitionSpec as P

TOPK = 8
MOST = 17
CHUNKS = 4
MESH = pl.DeviceIdType.MESH
SIDE_PARTS = ((), (3,), (1,), (4, 5))


def kernel(
    pipes,
    chips,
    sides,
    ids_ref,
    probs_ref,
    hidden_ref,
    sent_ref,
    head_ref,
    out_ref,
    tokens,
    metas,
    pick_a,
    pick_b,
    ids_in,
    probs_in,
    hidden_in,
    hidden,
    rows,
    acc,
    out_buf,
    own_sem,
    own_send,
    next_send,
    next_recv,
    prev_send,
    prev_recv,
    twin_send,
    twin_recv,
    side_send,
    side_recv,
    out_sem,
):
    tok, feat = sent_ref.shape
    piece = tok // CHUNKS
    half = chips // 2
    units = chips // 4
    block = 8 * tok
    pad_slots = rows.shape[1] // units
    lead = pick_a.shape[0]
    hid = hidden_ref.shape[1]

    me = lax.axis_index("expert")
    pipe = lax.axis_index("pipe")
    side = lax.axis_index("tensor")
    z = me // 2
    core = me % 2
    experts = 2 * chips
    to_next = {"expert": lax.rem(me + 2, experts)}
    to_prev = {"expert": lax.rem(me + experts - 2, experts)}
    to_twin = {"expert": me + 1 - 2 * core}
    turn = 1 - 2 * core
    right = lax.rem(side + sides + turn, sides)
    left = lax.rem(side + sides - turn, sides)
    to_right = {"tensor": right}
    to_left = {"tensor": left}
    to_lower = {"pipe": lax.rem(pipe + pipes - 1, pipes)}
    to_upper = {"pipe": lax.rem(pipe + 1, pipes)}

    def place_up(d):
        return 4 * (d // 2) + d % 2

    def place_down(d):
        return 4 * ((d - 1) // 2) + 2 + (d - 1) % 2

    def part(place, parity, index):
        start = pl.multiple_of((place * 2 + parity) * tok + index * piece, piece)
        return tokens.at[pl.ds(start, piece), :]

    def whole(place, parity):
        return tokens.at[pl.ds(pl.multiple_of((place * 2 + parity) * tok, tok), tok), :]

    def remote(src, dst, send, recv, device):
        return pltpu.make_async_remote_copy(
            src_ref=src,
            dst_ref=dst,
            send_sem=send,
            recv_sem=recv,
            device_id=device,
            device_id_type=MESH,
        )

    def own_local(index):
        span = pl.ds(index * piece, piece)
        return pltpu.make_async_copy(
            head_ref.at[span, :], part(0, core, index), own_sem.at[index]
        )

    def own_remote(index):
        span = pl.ds(index * piece, piece)
        return remote(
            sent_ref.at[span, :],
            part(0, core, index),
            own_send.at[index],
            own_sem.at[index],
            to_lower,
        )

    def ring(send, recv, device, src, dst, step, index):
        if index < CHUNKS:
            a, b = part(src, core, index), part(dst, core, index)
        else:
            a, b = metas.at[src * 2 + core], metas.at[dst * 2 + core]
        return remote(a, b, send.at[step % 2, index], recv.at[step + 1, index], device)

    def next_copy(step, index):
        src = place_down(step) if not isinstance(step, int) or step > 0 else 0
        return ring(next_send, next_recv, to_next, src, place_down(step + 1), step, index)

    def prev_copy(step, index):
        far = place_up(step + 1)
        dst = jnp.where(step + 1 == half, place_down(half), far)
        return ring(prev_send, prev_recv, to_prev, place_up(step), dst, step, index)

    def twin_copies(place, parity, way, slot):
        return (
            remote(
                whole(place, parity),
                whole(place, parity),
                twin_send.at[way, slot, 0],
                twin_recv.at[place, 0],
                to_twin,
            ),
            remote(
                metas.at[place * 2 + parity],
                metas.at[place * 2 + parity],
                twin_send.at[way, slot, 1],
                twin_recv.at[place, 1],
                to_twin,
            ),
        )

    def row_span(unit, start, size):
        return pl.ds(pl.multiple_of(unit * pad_slots + start, 16), size)

    def side_copy(unit, kind, which):
        if kind == 0:
            cut_a, cut_b = (0, lead // 2), (lead // 2, lead // 2)
        else:
            rest = pad_slots - lead
            size = (rest // 32) * 16 + (16 if rest % 32 else 0)
            cut_a, cut_b = (lead, size), (lead + size, rest - size)
        a, b = row_span(unit, *cut_a), row_span(unit, *cut_b)
        src, dst, span, device = (
            (0, 2, a, to_right),
            (0, 2, b, to_right),
            (0, 1, b, to_left),
            (0, 1, a, to_left),
            (2, 3, a, to_right),
            (1, 3, b, to_left),
        )[which]
        return remote(
            rows.at[src, span, :],
            rows.at[dst, span, :],
            side_send.at[unit, kind, which],
            side_recv.at[unit, kind, which],
            device,
        )

    own_ids = pltpu.make_async_copy(ids_ref, ids_in, out_sem.at[1])
    own_probs = pltpu.make_async_copy(probs_ref, probs_in, out_sem.at[2])
    own_hidden = pltpu.make_async_copy(hidden_ref, hidden_in, out_sem.at[0])
    own_ids.start()
    own_probs.start()
    own_hidden.start()
    own_ids.wait()
    own_probs.wait()
    metas[core] = jnp.concatenate(
        [ids_in[...].astype(jnp.float32), probs_in[...].astype(jnp.float32)], axis=0
    ).astype(metas.dtype)

    @pl.when(pipe == pipes - 1)
    def _():
        for index in range(CHUNKS):
            own_local(index).start()

    barrier = pltpu.get_barrier_semaphore()
    for device in (to_next, to_prev, to_twin, to_right, to_left, to_lower, to_upper):
        pl.semaphore_signal(barrier, inc=1, device_id=device, device_id_type=MESH)
    pl.semaphore_wait(barrier, 7)

    @pl.when(pipe > 0)
    def _():
        for index in range(CHUNKS):
            own_remote(index).start()

    next_copy(0, CHUNKS).start()
    prev_copy(0, CHUNKS).start()
    for index in range(CHUNKS):

        @pl.when(pipe == pipes - 1)
        def _():
            own_local(index).wait()

        @pl.when(pipe < pipes - 1)
        def _():
            own_remote(index).wait_recv()

        next_copy(0, index).start()
        prev_copy(0, index).start()
    for copy in twin_copies(0, core, 0, 0):
        copy.start()
    own_hidden.wait()

    before = (
        lax.broadcasted_iota(jnp.int32, (tok, tok), 0)
        < lax.broadcasted_iota(jnp.int32, (tok, tok), 1)
    ).astype(jnp.float32)
    mine = me.astype(jnp.float32)

    def twin_wait(unit, quarters):
        for q in quarters:
            for copy in twin_copies(4 * unit + q, 1 - core, 0, 0):
                copy.wait_recv()

    def mark(pick, unit, blocks, base):
        gates, hits = [], []
        for b in blocks:
            meta = metas[unit * 8 + b].astype(jnp.float32)
            hit = meta[:TOPK] == mine
            gates.append(jnp.sum(jnp.where(hit, meta[TOPK:], 0.0), axis=0, keepdims=True))
            hits.append(jnp.sum(jnp.where(hit, 1.0, 0.0), axis=0, keepdims=True))
        spare = jnp.zeros((8 - len(blocks), tok), jnp.float32)
        routed = jnp.concatenate([*hits, spare], axis=0)
        rank = jnp.dot(routed, before, preferred_element_type=jnp.float32)
        slots = (
            lax.broadcasted_iota(jnp.int32, (pick.shape[0], tok), 0) + base
        ).astype(jnp.float32)
        for n, b in enumerate(blocks):
            slot = jnp.where(routed[n : n + 1] > 0.5, rank[n : n + 1] + b * MOST, -1.0)
            pick[:, n * tok : (n + 1) * tok] = jnp.where(slots == slot, gates[n], 0.0).astype(
                pick.dtype
            )

    def prepare_a(unit):
        twin_wait(unit, (0, 1, 2))
        mark(pick_a, unit, range(6), 0)

    def permute(unit):
        total = hidden_in.shape[0]
        i = lax.broadcasted_iota(jnp.int32, (pad_slots, total), 0)
        width = 2 * MOST
        offsets = (2 * unit, 2 * unit + 1, chips - 2 * unit - 1, chips - 2 * unit - 2)
        target = jnp.full((pad_slots, total), -1, jnp.int32)
        for q in range(4):
            chip = lax.rem(z + offsets[q], chips)
            inside = (i >= q * width) & (i < (q + 1) * width)
            target = jnp.where(inside, i + (chip - q) * width, target)
        order = (lax.broadcasted_iota(jnp.int32, (pad_slots, total), 1) == target).astype(
            jnp.bfloat16
        )
        hidden[row_span(unit, 0, pad_slots), :] = jnp.dot(
            order, hidden_in[...], preferred_element_type=jnp.float32
        ).astype(jnp.bfloat16)

    def prepare_b(unit):
        twin_wait(unit, (3,))
        mark(pick_b, unit, range(5, 8), lead)

    def select(unit, kind, start, size):
        pick, base, skip = ((pick_a, 0, 0), (pick_b, lead, 5 * tok))[kind]
        span = pl.ds(pl.multiple_of(unit * block + skip, tok), pick.shape[1])
        rows[0, row_span(unit, base, pick.shape[0]), start : start + size] = jnp.dot(
            pick[...], tokens[span, start : start + size], preferred_element_type=jnp.float32
        ).astype(jnp.bfloat16)

    def send(unit, kind):
        for which in range(4):
            side_copy(unit, kind, which).start()

    def product(which, begin, end):
        span = slice(begin, end)
        return lax.dot_general(
            hidden[span, :],
            rows[which, span, :],
            (((0,), (0,)), ((), ())),
            preferred_element_type=jnp.float32,
        )

    def wait_sides(unit, kind, parts):
        for which in parts:
            side_copy(unit, kind, which).wait_recv()

    def settle(which, begin, end):
        for unit in range(begin, end):
            for kind in range(2):
                wait_sides(unit, kind, SIDE_PARTS[which])

    def forward(unit, kind):
        wait_sides(unit, kind, (0, 2))
        side_copy(unit, kind, 4).start()
        side_copy(unit, kind, 5).start()

    def arrived(recv, place, step, index):
        if index < CHUNKS:
            a = part(place, core, index)
        else:
            a = metas.at[place * 2 + core]
        remote(a, a, next_send.at[0, index], recv.at[step, index], to_next).wait_recv()

    cut = min(feat, 512)
    early = max(0, (half - 9) // 2 + 1)
    wide = cut < feat

    def advance(step, carry):
        even = lax.rem(step, 2) == 0
        unit_a = (step - 2) // 2
        unit_b = (step - 3) // 2
        busy_a = even & (step >= 2)
        busy_b = (lax.rem(step, 2) == 1) & (step >= 3)
        down = place_down(step)
        up = place_up(step)
        forward_next = (step < half - 1) | (core == 0)
        forward_prev = (step < half - 1) | (core == 1)
        for index in (CHUNKS, *range(CHUNKS)):
            arrived(next_recv, down, step, index)

            @pl.when(forward_next)
            def _():
                @pl.when(step >= 2)
                def _():
                    next_copy(step, index).wait_send()

                next_copy(step, index).start()

            arrived(prev_recv, up, step, index)

            @pl.when(forward_prev)
            def _():
                @pl.when(step >= 2)
                def _():
                    prev_copy(step, index).wait_send()

                prev_copy(step, index).start()

            if index == 0:

                @pl.when(busy_a & (step >= 4))
                def _():
                    forward(unit_a - 1, 0)

                @pl.when(busy_a)
                def _():
                    prepare_a(unit_a)
                    permute(unit_a)

                @pl.when(busy_b & (step >= 5))
                def _():
                    forward(unit_b - 1, 1)

                @pl.when(busy_b)
                def _():
                    prepare_b(unit_b)

            for kind, busy, unit in ((0, busy_a, unit_a), (1, busy_b, unit_b)):
                if index == 1:

                    @pl.when(busy)
                    def _():
                        select(unit, kind, 0, cut)

                if index == 2:

                    @pl.when(busy)
                    def _():
                        if wide:
                            select(unit, kind, cut, feat - cut)
                        send(unit, kind)

            if early and index < 4:

                @pl.when(step == half - 2)
                def _():
                    settle(index, 0, early)
                    acc[index] = product(index, 0, early * pad_slots)

        @pl.when(step >= 2)
        def _():
            for copy in twin_copies(down, core, 0, step % 2):
                copy.wait_send()

        for copy in twin_copies(down, core, 0, step % 2):
            copy.start()

        @pl.when(step >= 3)
        def _():
            for copy in twin_copies(up, core, 1, step % 2):
                copy.wait_send()

        for copy in twin_copies(up, core, 1, step % 2):
            copy.start()
        return carry

    lax.fori_loop(1, half, advance, 0)

    def finish(unit, kind):
        (prepare_a, prepare_b)[kind](unit)
        select(unit, kind, 0, cut)
        if wide:
            select(unit, kind, cut, feat - cut)
        send(unit, kind)

    if units > 1:
        forward(units - 2, 0)
    finish(units - 1, 0)

    last = place_down(half)
    for way, recv in ((0, next_recv), (1, prev_recv)):

        @pl.when(core == way)
        def _():
            for index in (CHUNKS, *range(CHUNKS)):
                arrived(recv, last, half, index)
            for copy in twin_copies(last, core, way, half % 2):
                copy.wait_send()
            for copy in twin_copies(last, core, way, half % 2):
                copy.start()

    late = max(early, units - 2)
    split = (units - 1) * pad_slots + lead
    if units > 1:
        forward(units - 2, 1)
    permute(units - 1)
    if late > early:
        for which in range(4):
            settle(which, early, late)
            more = product(which, early * pad_slots, late * pad_slots)
            acc[which] = acc[which] + more if early else more
    finish(units - 1, 1)

    def gather_up(which):
        settle(which, late, units - 1)
        wait_sides(units - 1, 0, SIDE_PARTS[which])
        more = product(which, late * pad_slots, split)
        acc[which] = acc[which] + more if late else more

    forward(units - 1, 0)
    for which in range(3):
        gather_up(which)
    forward(units - 1, 1)
    gather_up(3)
    for which in range(4):
        wait_sides(units - 1, 1, SIDE_PARTS[which])
        total = acc[which] + product(which, split, units * pad_slots)
        out_buf[which] = total.astype(out_buf.dtype)
        owner = (side, right, left, lax.rem(side + 2, sides))[which]
        columns = pl.ds(pl.multiple_of(owner * feat, 128), feat)
        pltpu.make_async_copy(out_buf.at[which], out_ref.at[:, columns], out_sem.at[which]).start()

    for index in range(CHUNKS + 1):
        for parity in range(2):
            next_copy(half - 2 + parity, index).wait_send()
            prev_copy(half - 2 + parity, index).wait_send()
    for way in range(2):
        for parity in range(2):
            for copy in twin_copies(0, core, way, parity):
                copy.wait_send()

    def drain(unit, carry):
        for kind in range(2):
            for which in range(6):
                side_copy(unit, kind, which).wait_send()
        return carry

    lax.fori_loop(0, units, drain, 0)

    @pl.when(pipe > 0)
    def _():
        for index in range(CHUNKS):
            own_remote(index).wait_send()

    for which in range(4):
        pltpu.make_async_copy(
            out_buf.at[which], out_ref.at[:, pl.ds(0, feat)], out_sem.at[which]
        ).wait()


def local(sent_grad, head_grad, probs, expert_ids, hidden_act):
    pipes = lax.axis_size("pipe")
    experts = lax.axis_size("expert")
    sides = lax.axis_size("tensor")
    chips = experts // 2
    half = chips // 2
    units = chips // 4
    tok, feat = head_grad.shape
    hid = hidden_act.shape[3]
    pad_slots = -(-8 * MOST // 16) * 16
    lead = 96
    bf16 = jnp.bfloat16
    dma = pltpu.SemaphoreType.DMA
    vmem = pl.BlockSpec(memory_space=pltpu.VMEM)
    anywhere = pl.BlockSpec(memory_space=pl.ANY)
    hbm = pl.BlockSpec(memory_space=pltpu.HBM)
    grad = pl.pallas_call(
        functools.partial(kernel, pipes, chips, sides),
        out_shape=jax.ShapeDtypeStruct((hid, sides * feat), bf16),
        in_specs=[hbm, hbm, hbm, hbm, hbm],
        out_specs=anywhere,
        scratch_shapes=[
            pltpu.VMEM((experts * tok, feat), bf16),
            pltpu.VMEM((experts, 2 * TOPK, tok), bf16),
            pltpu.VMEM((lead, 6 * tok), bf16),
            pltpu.VMEM((pad_slots - lead, 3 * tok), bf16),
            pltpu.VMEM((TOPK, tok), jnp.int32),
            pltpu.VMEM((TOPK, tok), bf16),
            pltpu.VMEM(hidden_act.shape[2:], bf16),
            pltpu.VMEM((units * pad_slots, hid), bf16),
            pltpu.VMEM((4, units * pad_slots, feat), bf16),
            pltpu.VMEM((4, hid, feat), jnp.float32),
            pltpu.VMEM((4, hid, feat), bf16),
            dma((CHUNKS,)),
            dma((CHUNKS,)),
            dma((2, CHUNKS + 1)),
            dma((half + 1, CHUNKS + 1)),
            dma((2, CHUNKS + 1)),
            dma((half + 1, CHUNKS + 1)),
            dma((2, 2, 2)),
            dma((chips, 2)),
            dma((units, 2, 6)),
            dma((units, 2, 6)),
            dma((4,)),
        ],
        compiler_params=pltpu.CompilerParams(
            collective_id=0, has_side_effects=True, vmem_limit_bytes=36_000_000
        ),
    )(*(pltpu.with_memory_space_constraint(a, pltpu.HBM) for a in (expert_ids[0].T, probs[0].T, hidden_act[0, 0], sent_grad[0], head_grad)))
    return grad[None, None]


def solution(mesh):
    in_specs = (
        P("pipe", "expert", "tensor"),
        P("expert", "tensor"),
        P("pipe", "expert", None),
        P("pipe", "expert", None),
        P("pipe", "expert", None, "tensor"),
    )
    out_specs = P("pipe", "expert", "tensor", None)
    return jax.shard_map(local, mesh=mesh, in_specs=in_specs, out_specs=out_specs, check_vma=False)
```
